32 devices in a mesh: ty: 8 (over z, y), tx: 4 (over x, core).
Axes of the slice: x: 2, y: 2, z: 4, core: 2. Of those that a mesh axis runs over, the one named last changes fastest.
Arguments:
- density: bfloat16 [8, 256, 1024], P(None, 'ty', 'tx'), may hold values from 0 to 2
- stem_weight: bfloat16 [256, 72], replicated, may hold values from -0.75 to 0.75
- down_weight: bfloat16 [4, 512, 256], replicated, may hold values from -0.1875 to 0.1875
- depth_kernel: float32 [512, 7, 7], replicated, may hold values from -0.875 to 0.875
- mix_weight: bfloat16 [512, 512], replicated, may hold values from -0.25 to 0.25
- up_weight: bfloat16 [4, 256, 512], replicated, may hold values from -0.25 to 0.25
- head_weight: bfloat16 [4, 256], replicated, may hold values from -0.375 to 0.375
- cotangent: bfloat16 [4, 256, 1024], P(None, 'ty', 'tx'), may hold values from -24 to 24
- send_blocks: int32 [32, 128], P(('ty', 'tx')), may hold values from 0 to 255
- cell_slot: int32 [65536], P(('ty', 'tx')), may hold values from 0 to 127
- cell_offset: int32 [65536], P(('ty', 'tx')), may hold values from 0 to 127
- cell_area: float32 [65536], P(('ty', 'tx')), may hold values from 0.5 to 4
Outputs:
- congestion: bfloat16 [4, 256, 1024], P(None, 'ty', 'tx')
- cell_grad: float32 [65536], P(('ty', 'tx'))
The draws below stay inside these ranges and needn't reach their ends.
Inputs may be any that keep to these rules, and one draw needn't show every extreme that they name: `send_blocks`: a local bin block index of the sending device. `cell_slot`: slots read by a cell; a few sending devices are read by many cells.
All inputs are finite; a program needn't handle non-finite values.
Results may differ from the reference program's by a relative error of at most 0.014.
Values may be sent and summed in bfloat16 or wider, within the bound.
No kernel may reach another device: no remote copies, remote signals or barrier semaphores. Data moves between devices by JAX's collectives and lax.ppermute only.
A program may use at most 192 MiB of HBM per device.

```python
import math
import jax
import jax.numpy as jnp
import numpy as np

NDIE = 4
CIN = 8
C3 = 256
C4 = 512
HT = 32
WT = 256
CAP = 4
CELLS_DEV = 2048
NH = 256
NW = 1024
CELLS = 65536
N_TY = 8
N_TX = 4


def plant(drawn, stream_key, smallest, top_value):
    longest = drawn.shape.index(max(drawn.shape))
    spots = []
    for shift in (0, 1):
        where = [jax.random.randint(jax.random.fold_in(stream_key, axis), (), 0, length) for axis, length in enumerate(drawn.shape)]
        where[longest] = (where[longest] + shift) % drawn.shape[longest]
        spots.append(tuple(where))
    return drawn.at[spots[0]].set(smallest).at[spots[1]].set(top_value)


def block_levels(key, extent, shards, low, largest):
    level, own = 1.0, jax.random.fold_in(key, 6)
    for axis_at, blocks in shards:
        heights = jnp.exp(jax.random.uniform(jax.random.fold_in(own, axis_at), (blocks,), jnp.float32, low / len(shards), largest / len(shards)))
        level = level * jnp.repeat(heights, extent[axis_at] // blocks).reshape([-1 if axis == axis_at else 1 for axis in range(len(extent))])
    return level


def rank_table(number_of, slope):
    loads = [(1 << 20) // math.isqrt(standing ** slope) + 1 for standing in range(1, number_of + 1)]
    width = 1 + sum(loads) // (1 << 30)
    return np.cumsum(np.array([max(1, weight // width) for weight in loads]))


def skewed_ids(own_key, dims, amount, lean):
    listing = rank_table(amount, lean)
    lot = jax.random.randint(jax.random.fold_in(own_key, 1), dims, 0, int(listing[amount - 1]))
    grade = jnp.searchsorted(jnp.asarray(listing, jnp.int32), lot, side="right")
    return jax.random.permutation(jax.random.fold_in(own_key, 2), amount)[grade].astype(jnp.int32)


def centred(stream_key, extent, spread, reach, split=(), held_as=jnp.bfloat16):
    level = block_levels(stream_key, extent, split, -0.22, 0.18) if split else 1.0
    values = jax.random.normal(stream_key, extent, jnp.float32) * spread * level
    return jnp.minimum(jnp.maximum(values, -reach), reach).astype(held_as)


def setup_inputs(seed: int = 0) -> dict:
    streams_of = jax.random.split(jax.random.key(seed), 13)
    density = jnp.clip(2.0 * jax.random.uniform(streams_of[0], (CIN, NH, NW), jnp.float32) ** block_levels(streams_of[0], (CIN, NH, NW), ((1, 8), (2, 4)), -0.2, 0.2), 0.0, 2.0).astype(jnp.bfloat16)
    stem_weight = centred(streams_of[1], (C3, 9 * CIN), (9 * CIN) ** -0.5, 0.75)
    down_weight = centred(streams_of[2], (4, C4, C3), (4 * C3) ** -0.5, 0.1875)
    depth_kernel = centred(streams_of[3], (C4, 7, 7), 49 ** -0.5, 0.875, (), jnp.float32)
    mix_weight = centred(streams_of[4], (C4, C4), C4 ** -0.5, 0.25)
    up_weight = centred(streams_of[5], (4, C3, C4), C4 ** -0.5, 0.25)
    head_weight = centred(streams_of[6], (NDIE, C3), C3 ** -0.5, 0.375)
    cotangent = centred(streams_of[7], (NDIE, NH, NW), 4.0, 24.0, ((1, 8), (2, 4)))
    send_blocks = plant(jax.random.randint(streams_of[8], (N_TY * N_TX, N_TY * N_TX * CAP), 0, NDIE * HT * WT // 128), jax.random.fold_in(streams_of[8], 1), 0, (NDIE * HT * WT // 128) - 1).astype(jnp.int32)
    cell_slot = plant(skewed_ids(streams_of[9], (CELLS,), N_TY * N_TX * CAP, 1), jax.random.fold_in(streams_of[9], 3), 0, (N_TY * N_TX * CAP) - 1).astype(jnp.int32)
    cell_offset = plant(jax.random.randint(streams_of[10], (CELLS,), 0, 128), jax.random.fold_in(streams_of[10], 1), 0, 127).astype(jnp.int32)
    cell_area = jnp.clip(jnp.exp(math.log(4.0) - 2.0794415 * jax.random.uniform(streams_of[11], (CELLS,), jnp.float32) ** block_levels(streams_of[11], (CELLS,), ((0, 32),), -0.2, 0.2)), 0.5, 4.0)
    return dict(density=density, stem_weight=stem_weight, down_weight=down_weight, depth_kernel=depth_kernel, mix_weight=mix_weight, up_weight=up_weight, head_weight=head_weight, cotangent=cotangent, send_blocks=send_blocks, cell_slot=cell_slot, cell_offset=cell_offset, cell_area=cell_area)


def silu_slope(value):
    sigma = jax.nn.sigmoid(value)
    return sigma * (1.0 + value * (1.0 - sigma))


def stem_conv(padded, stem_weight):
    height = padded.shape[1] - 2
    breadth = padded.shape[2] - 2
    patches = jnp.concatenate([padded[:, row_tap:row_tap + height, col_tap:col_tap + breadth] for row_tap in range(3) for col_tap in range(3)], axis=0)
    result = jnp.dot(stem_weight, patches.reshape(patches.shape[0], -1), preferred_element_type=jnp.float32)
    return result.reshape(stem_weight.shape[0], height, breadth)


def stride_down(feature_map, weights, transposed):
    total = None
    for corner in range(4):
        matrix = weights[corner].T if transposed else weights[corner]
        picked = feature_map[:, corner // 2::2, corner % 2::2]
        term = jnp.dot(matrix, picked.reshape(picked.shape[0], -1), preferred_element_type=jnp.float32)
        total = term if total is None else total + term
    return total.reshape(total.shape[0], feature_map.shape[1] // 2, feature_map.shape[2] // 2)


def stride_up(feature_map, weights, transposed):
    flat = feature_map.reshape(feature_map.shape[0], -1)
    parts = []
    for corner in range(4):
        matrix = weights[corner].T if transposed else weights[corner]
        parts.append(jnp.dot(matrix, flat, preferred_element_type=jnp.float32))
    outputs = parts[0].shape[0]
    stacked = jnp.stack(parts).reshape(2, 2, outputs, feature_map.shape[1], feature_map.shape[2])
    return stacked.transpose(2, 3, 0, 4, 1).reshape(outputs, 2 * feature_map.shape[1], 2 * feature_map.shape[2])


def depthwise(padded, kernel):
    height = padded.shape[1] - 6
    breadth = padded.shape[2] - 6
    total = jnp.zeros((padded.shape[0], height, breadth), jnp.float32)
    for row_tap in range(7):
        for col_tap in range(7):
            total = total + kernel[:, row_tap, col_tap][:, None, None] * padded[:, row_tap:row_tap + height, col_tap:col_tap + breadth]
    return total


def pad_map(feature_map, margin):
    return jnp.pad(feature_map, ((0, 0), (margin, margin), (margin, margin)))


def reference(density, stem_weight, down_weight, depth_kernel, mix_weight, up_weight, head_weight, cotangent, send_blocks, cell_slot, cell_offset, cell_area):
    features_pre = stem_conv(pad_map(density, 1), stem_weight)
    features = jax.nn.silu(features_pre).astype(jnp.bfloat16)
    coarse_pre = stride_down(features, down_weight, False)
    coarse = jax.nn.silu(coarse_pre).astype(jnp.bfloat16)
    mixed = (coarse + depthwise(pad_map(coarse, 3), depth_kernel)).astype(jnp.bfloat16)
    channels, half_rows, half_cols = coarse.shape
    hidden_pre = jnp.dot(mix_weight, mixed.reshape(channels, -1), preferred_element_type=jnp.float32).reshape(channels, half_rows, half_cols)
    hidden_map = jax.nn.silu(hidden_pre).astype(jnp.bfloat16)
    skipped_pre = stride_up(hidden_map, up_weight, False) + features
    skipped = jax.nn.silu(skipped_pre).astype(jnp.bfloat16)
    wide, map_rows, map_cols = skipped.shape
    dies = head_weight.shape[0]
    congestion = jnp.dot(head_weight, skipped.reshape(wide, -1), preferred_element_type=jnp.float32).reshape(dies, map_rows, map_cols).astype(jnp.bfloat16)
    head_back = jnp.dot(head_weight.T, cotangent.reshape(dies, -1), preferred_element_type=jnp.float32).reshape(wide, map_rows, map_cols)
    grad_skip = (silu_slope(skipped_pre) * head_back).astype(jnp.bfloat16)
    grad_hidden = (silu_slope(hidden_pre) * stride_down(grad_skip, up_weight, True)).astype(jnp.bfloat16)
    grad_mixed = jnp.dot(mix_weight.T, grad_hidden.reshape(channels, -1), preferred_element_type=jnp.float32).reshape(channels, half_rows, half_cols).astype(jnp.bfloat16)
    flipped = depth_kernel[:, ::-1, ::-1]
    coarse_back = (grad_mixed + depthwise(pad_map(grad_mixed, 3), flipped)).astype(jnp.bfloat16)
    grad_coarse = (silu_slope(coarse_pre) * coarse_back).astype(jnp.bfloat16)
    grad_features = (silu_slope(features_pre) * (grad_skip + stride_up(grad_coarse, down_weight, True))).astype(jnp.bfloat16)
    in_maps = stem_weight.shape[1] // 9
    tap_weight = stem_weight.reshape(wide, 9, in_maps)[:, :, 0::2].reshape(wide, 9 * dies)
    taps = jnp.dot(tap_weight.T, grad_features.reshape(wide, -1), preferred_element_type=jnp.float32).reshape(9 * dies, map_rows, map_cols)
    taps = pad_map(taps, 1).reshape(9, dies, map_rows + 2, map_cols + 2)
    grad_bins = jnp.zeros((dies, map_rows, map_cols), jnp.float32)
    for row_tap in range(3):
        for col_tap in range(3):
            grad_bins = grad_bins + taps[3 * row_tap + col_tap][:, 2 - row_tap:2 - row_tap + map_rows, 2 - col_tap:2 - col_tap + map_cols]
    owners = jnp.arange(CELLS, dtype=jnp.int32) // CELLS_DEV
    source = cell_slot // CAP
    column_slot = owners * CAP + cell_slot % CAP
    block_id = send_blocks[source, column_slot]
    per_die = HT * WT // 128
    cell_die = block_id // per_die
    inside = (block_id % per_die) * 128 + cell_offset
    bin_row = (source // N_TX) * HT + inside // WT
    bin_column = (source % N_TX) * WT + inside % WT
    cell_grad = cell_area * grad_bins[cell_die, bin_row, bin_column]
    return congestion, cell_grad
```

```python
import functools

import jax
import jax.numpy as jnp
import numpy as np
from jax import lax
from jax.experimental import pallas as pl
from jax.experimental.pallas import tpu as pltpu
from jax.sharding import PartitionSpec as P


REACH = 7
MIDDLE = 4
EDGE = 1
MARGIN = 8
GUARD = 8
CHUNK = 3
ROW_ORDER = (1, 2, 3, 0)

NT = (((1,), (1,)), ((), ()))
f32 = jnp.float32
bf16 = jnp.bfloat16


def dot(a, b):
    return jnp.dot(a, b, preferred_element_type=f32)


def dot_nt(a, b):
    return lax.dot_general(a, b, NT, preferred_element_type=f32)


def sigmoid(value):
    return 0.5 * jnp.tanh(0.5 * value) + 0.5


def stem_selectors(maps, dies):
    table = np.zeros((4, 16 * maps + 16 * dies, 9 * maps), np.float32)
    for p in range(2):
        for q in range(2):
            tap = 2 * p + q
            for a in range(3):
                for b in range(3):
                    r, s = p + a, q + b
                    for c in range(maps):
                        table[tap, s * 4 * maps + r * maps + c, 3 * maps * a + maps * b + c] = 1
                    for k in range(dies):
                        row = 16 * maps + s * 4 * dies + ROW_ORDER.index(r) * dies + k
                        table[tap, row, 3 * maps * a + maps * b + 2 * k] = 1
    return table


def head_selectors(dies):
    table = np.zeros((4, 4 * dies, dies), np.float32)
    for p in range(2):
        for q in range(2):
            for k in range(dies):
                table[2 * p + q, q * 2 * dies + p * dies + k, k] = 1
    return table


def body(
    rows,
    cols,
    dies,
    maps,
    place_ref,
    x_ref,
    xh_ref,
    c_ref,
    ch_ref,
    w1_ref,
    hb_ref,
    dw_ref,
    down_t_ref,
    down_ref,
    mix_t_ref,
    mix_ref,
    up_t_ref,
    up_ref,
    cong_ref,
    bins_ref,
    sel_scr,
    spread_scr,
    mask_scr,
    p_scr,
    feat_scr,
    cpre_scr,
    coarse_scr,
    mixed_scr,
    gskip_scr,
    gmix_scr,
    back_scr,
    cong_scr,
    tap_scr,
    z_scr,
):
    wide = cols + 2 * MARGIN
    span = CHUNK * wide
    lanes = x_ref.shape[1] + xh_ref.shape[1]
    blocks = mix_ref.shape[0] // 128
    width = 2 * cols
    n_full = (rows + 2 * REACH) // CHUNK
    n_mid = (rows + 2 * MIDDLE) // CHUNK
    n_edge = (rows + 2 * EDGE) // CHUNK

    j = lax.broadcasted_iota(jnp.int32, (wide, lanes), 0)
    at = lax.broadcasted_iota(jnp.int32, (wide, lanes), 1)
    want = 2 * (j - MARGIN)
    want = jnp.where(want < 0, want + lanes, want)
    sel_scr[...] = jnp.where(at == want, 1.0, 0.0).astype(bf16)
    j = lax.broadcasted_iota(jnp.int32, (wide, width), 0)
    at = lax.broadcasted_iota(jnp.int32, (wide, width), 1)
    for s in range(4):
        spread_scr[s] = jnp.where(at == 2 * (j - MARGIN) - 1 + s, 1.0, 0.0).astype(bf16)
    column = lax.broadcasted_iota(jnp.int32, (wide, 128), 0) + place_ref[1] - MARGIN
    mask_scr[...] = jnp.where((column >= 0) & (column < place_ref[3]), 1.0, 0.0)
    for scr in (coarse_scr, gmix_scr):
        zero = jnp.zeros((blocks, scr.shape[1], GUARD, 128), f32)
        scr[:, :, 0:GUARD, :] = zero
        scr[:, :, GUARD + wide : 2 * GUARD + wide, :] = zero

    def row_valid(row):
        where = place_ref[0] + row
        inside = (where >= 0) & (where < place_ref[2])
        return jnp.where(inside, 1.0, 0.0).astype(f32)

    def patch_row(ii, carry):
        start = pl.multiple_of(16 * ii + 8, 8)
        part = jnp.concatenate(
            [x_ref[pl.ds(start, 4 * maps), :], xh_ref[pl.ds(start, 4 * maps), :]], axis=1
        )
        shifted = [part if s == 1 else pltpu.roll(part, (1 - s) % lanes, 1) for s in range(4)]
        stacked = jnp.concatenate(shifted, axis=0).astype(bf16)
        p_scr[pl.ds(pl.multiple_of(ii * wide, 16), wide), :] = dot_nt(
            sel_scr[...], stacked
        ).astype(bf16)
        return carry

    lax.fori_loop(0, rows + 2 * REACH, patch_row, 0)

    def first(ch, carry):
        base = pl.multiple_of(ch * span, 16)
        patches = p_scr[pl.ds(base, span), :]
        total = None
        for tap in range(4):
            pre = dot(patches, w1_ref[tap, 0 : 16 * maps, :])
            feat = (pre * sigmoid(pre)).astype(bf16)
            feat_scr[pl.ds(base, span), tap * 256 : (tap + 1) * 256] = feat
            term = dot(feat, down_t_ref[tap])
            total = term if total is None else total + term
        cpre_scr[pl.ds(base, span), :] = total
        coarse = (total * sigmoid(total)).astype(bf16).astype(f32)
        for r in range(CHUNK):
            row = ch * CHUNK + r
            mask = mask_scr[...] * row_valid(row - REACH)
            for b in range(blocks):
                coarse_scr[b, row, GUARD : GUARD + wide, :] = (
                    coarse[r * wide : (r + 1) * wide, b * 128 : (b + 1) * 128] * mask
                )
        return carry

    lax.fori_loop(0, n_full, first, 0)

    def depthwise(src, dst, ch, flipped):
        for b in range(blocks):

            def columns(cb, carry):
                start = cb * 16
                total = [[None, None] for _ in range(CHUNK)]
                for q in range(7):
                    for ri in range(CHUNK + 6):
                        for h in range(2):
                            at = start + (8 * h + q + GUARD - 3)
                            piece = src[b, ch * CHUNK + ri, pl.ds(at, 8), :]
                            for r in range(CHUNK):
                                p = ri - r
                                if 0 <= p < 7:
                                    tap = 7 * p + q
                                    weight = dw_ref[b, 48 - tap if flipped else tap]
                                    term = weight * piece
                                    old = total[r][h]
                                    total[r][h] = term if old is None else old + term
                for r in range(CHUNK):
                    where = pl.multiple_of(r * wide + start, 16)
                    dst[pl.ds(where, 16), b * 128 : (b + 1) * 128] = jnp.concatenate(
                        total[r], axis=0
                    ).astype(bf16)
                return carry

            lax.fori_loop(0, wide // 16, columns, 0)

    def middle(ch, carry):
        depthwise(coarse_scr, mixed_scr, ch, False)
        hidden_pre = dot(mixed_scr[...], mix_t_ref[...])
        s = sigmoid(hidden_pre)
        hidden = hidden_pre * s
        slope_hidden = s + hidden * (1.0 - s)
        hidden = hidden.astype(bf16)
        cot = []
        for r in range(CHUNK):
            at = pl.multiple_of((ch * CHUNK + r) * 2 * dies, 8)
            part = jnp.concatenate(
                [c_ref[pl.ds(at, 2 * dies), :], ch_ref[pl.ds(at, 2 * dies), :]], axis=1
            )
            part = jnp.concatenate([part, pltpu.roll(part, lanes - 1, 1)], axis=0).astype(bf16)
            cot.append(dot_nt(sel_scr[...], part).astype(bf16))
        cot = jnp.concatenate(cot, axis=0)
        base = pl.multiple_of(ch * span, 16)
        at_feat = pl.multiple_of((ch + (REACH - MIDDLE) // CHUNK) * span, 16)
        grad = None
        congestion = [None] * CHUNK
        for tap in range(4):
            lane = slice(tap * 256, (tap + 1) * 256)
            pre = dot(hidden, up_t_ref[tap]) + feat_scr[pl.ds(at_feat, span), lane].astype(f32)
            s = sigmoid(pre)
            act = pre * s
            slope = s + act * (1.0 - s)
            act = act.astype(bf16)
            for r in range(CHUNK):
                term = dot_nt(hb_ref[tap], act[r * wide : (r + 1) * wide])
                congestion[r] = term if tap == 0 else congestion[r] + term
            gskip = (slope * dot(cot, hb_ref[tap])).astype(bf16)
            gskip_scr[pl.ds(base, span), lane] = gskip
            term = dot(gskip, up_ref[tap])
            grad = term if grad is None else grad + term
        for r in range(CHUNK):
            at = pl.multiple_of((ch * CHUNK + r) * 2 * dies, 8)
            for q in range(2):
                cong_scr[q, pl.ds(at, 2 * dies), 0:wide] = congestion[r][
                    q * 2 * dies : (q + 1) * 2 * dies
                ]
        ghidden = (slope_hidden * grad).astype(bf16)
        gmix = dot(ghidden, mix_ref[...]).astype(bf16).astype(f32)
        for r in range(CHUNK):
            for b in range(blocks):
                gmix_scr[b, ch * CHUNK + r, GUARD : GUARD + wide, :] = gmix[
                    r * wide : (r + 1) * wide, b * 128 : (b + 1) * 128
                ]
        return carry

    lax.fori_loop(0, n_mid, middle, 0)

    def last(ch, carry):
        depthwise(gmix_scr, back_scr, ch, True)
        base = pl.multiple_of((ch + (REACH - EDGE) // CHUNK) * span, 16)
        at_skip = pl.multiple_of((ch + (MIDDLE - EDGE) // CHUNK) * span, 16)
        pre = cpre_scr[pl.ds(base, span), :]
        s = sigmoid(pre)
        slope = s + pre * s * (1.0 - s)
        grad = slope * back_scr[...].astype(f32)
        masked = []
        for r in range(CHUNK):
            mask = mask_scr[...] * row_valid(ch * CHUNK + r - EDGE)
            mask = jnp.concatenate([mask] * blocks, axis=1)
            masked.append((grad[r * wide : (r + 1) * wide] * mask).astype(bf16))
        grad = jnp.concatenate(masked, axis=0)
        patches = p_scr[pl.ds(base, span), :]
        taps = [None] * CHUNK
        for tap in range(4):
            lane = slice(tap * 256, (tap + 1) * 256)
            pre = dot(patches, w1_ref[tap, 0 : 16 * maps, :])
            s = sigmoid(pre)
            slope = s + pre * s * (1.0 - s)
            total = gskip_scr[pl.ds(at_skip, span), lane].astype(f32) + dot(grad, down_ref[tap])
            gfeat = (slope * total).astype(bf16)
            weight = w1_ref[tap, 16 * maps : 16 * maps + 16 * dies, :]
            for r in range(CHUNK):
                term = dot_nt(weight, gfeat[r * wide : (r + 1) * wide])
                taps[r] = term if tap == 0 else taps[r] + term
        for r in range(CHUNK):
            high = taps[r].astype(bf16)
            low = (taps[r] - high.astype(f32)).astype(bf16)
            at = pl.multiple_of((ch * CHUNK + r) * 8 * dies, 16)
            for s in range(4):
                piece = slice(s * 4 * dies, (s + 1) * 4 * dies)
                tap_scr[s, pl.ds(at, 4 * dies), 0:wide] = high[piece]
                tap_scr[s, pl.ds(at + 4 * dies, 4 * dies), 0:wide] = low[piece]
        return carry

    lax.fori_loop(0, n_edge, last, 0)

    own = slice(MIDDLE * 2 * dies, (MIDDLE + rows) * 2 * dies)
    cong_ref[...] = (
        dot(cong_scr[0, own, 0:wide].astype(bf16), spread_scr[1])
        + dot(cong_scr[1, own, 0:wide].astype(bf16), spread_scr[2])
    ).astype(bf16)
    z = None
    for s in range(4):
        term = dot(tap_scr[s, :, 0:wide], spread_scr[s])
        z = term if z is None else z + term
    z_scr[...] = z
    lower = lax.broadcasted_iota(jnp.int32, (2 * dies, width), 0) < dies
    step, half = (8 * dies, 4 * dies)

    def rim(i, first_row):
        at = i * step + first_row
        return z_scr[at : at + 2 * dies, :] + z_scr[at + half : at + half + 2 * dies, :]

    for i in range(rows):
        row = rim(i + EDGE, 0) + jnp.where(
            lower, rim(i + EDGE - 1, 2 * dies), rim(i + EDGE + 1, 2 * dies)
        )
        for h in range(width // 128):
            bins_ref[h, i * 2 * dies : (i + 1) * 2 * dies, :] = row[:, h * 128 : (h + 1) * 128]


def network(place, x, xh, c, ch, w1, hb, dw, down_t, down, mix_t, mix, up_t, up, rows, cols):
    dies, maps = (hb.shape[1] // 4, 8)
    wide = cols + 2 * MARGIN
    span = CHUNK * wide
    full, mid, edge = (rows + 2 * REACH, rows + 2 * MIDDLE, rows + 2 * EDGE)
    lanes = x.shape[1] + xh.shape[1]
    channels = mix.shape[0]
    blocks = channels // 128
    guarded = wide + 2 * GUARD
    vmem = pl.BlockSpec(memory_space=pltpu.VMEM)
    return pl.pallas_call(
        functools.partial(body, rows, cols, dies, maps),
        out_shape=(
            jax.ShapeDtypeStruct((rows * 2 * dies, 2 * cols), bf16),
            jax.ShapeDtypeStruct((2 * cols // 128, rows * 2 * dies, 128), f32),
        ),
        in_specs=[pl.BlockSpec(memory_space=pltpu.SMEM)] + [vmem] * 13,
        out_specs=(vmem, vmem),
        scratch_shapes=[
            pltpu.VMEM((wide, lanes), bf16),
            pltpu.VMEM((4, wide, 2 * cols), bf16),
            pltpu.VMEM((wide, 128), f32),
            pltpu.VMEM((full * wide, 16 * maps), bf16),
            pltpu.VMEM((full * wide, 1024), bf16),
            pltpu.VMEM((full * wide, channels), f32),
            pltpu.VMEM((blocks, full, guarded, 128), f32),
            pltpu.VMEM((span, channels), bf16),
            pltpu.VMEM((mid * wide, 1024), bf16),
            pltpu.VMEM((blocks, mid, guarded, 128), f32),
            pltpu.VMEM((span, channels), bf16),
            pltpu.VMEM((2, mid * 2 * dies, 256), f32),
            pltpu.VMEM((4, edge * 8 * dies, 256), bf16),
            pltpu.VMEM((edge * 8 * dies, 2 * cols), f32),
        ],
        compiler_params=pltpu.CompilerParams(vmem_limit_bytes=63_000_000),
        name="network",
    )(place, x, xh, c, ch, w1, hb, dw, down_t, down, mix_t, mix, up_t, up)


def shift(values, axis, forward):
    size = lax.axis_size(axis)
    pairs = [(i, i + 1) if forward else (i + 1, i) for i in range(size - 1)]
    return lax.ppermute(values, axis, pairs)


def local(
    density,
    stem_weight,
    down_weight,
    depth_kernel,
    mix_weight,
    up_weight,
    head_weight,
    cotangent,
    send_blocks,
    cell_slot,
    cell_offset,
    cell_area,
):
    maps, tile_rows, tile_cols = density.shape
    dies, wide = head_weight.shape
    rows, cols = (tile_rows // 2, tile_cols // 2)
    channels = mix_weight.shape[0]
    blocks = channels // 128
    dens = jnp.transpose(density, (1, 0, 2))
    cot = jnp.transpose(cotangent, (1, 0, 2)).reshape(rows, 2 * dies, tile_cols)
    deep, shallow = (2 * (REACH + 1), MIDDLE)
    last = jnp.concatenate([dens[-deep:], cot[-shallow:]], axis=0)
    first = jnp.concatenate([dens[:deep], cot[:shallow]], axis=0)
    above = shift(last, "ty", True)
    below = shift(first, "ty", False)
    main = jnp.concatenate(
        [above[:deep], dens, below[:deep], above[deep:], cot, below[deep:]], axis=0
    )
    side = 2 * MARGIN
    left = shift(main[:, :, -side:], "tx", True)
    right = shift(main[:, :, :side], "tx", False)
    gap = jnp.zeros(main.shape[:2] + (128 - 2 * side,), main.dtype)
    rim = jnp.concatenate([right, gap, left], axis=2)
    deep_rows = tile_rows + 2 * deep
    main = main.astype(f32)
    rim = rim.astype(f32)
    x = main[:deep_rows].reshape(-1, tile_cols)
    xh = rim[:deep_rows].reshape(-1, 128)
    c = main[deep_rows:].reshape(-1, tile_cols)
    ch = rim[deep_rows:].reshape(-1, 128)
    stem_table = jnp.asarray(stem_selectors(maps, dies), bf16)
    w1 = jnp.einsum("tsk,ok->tso", stem_table, stem_weight, preferred_element_type=f32).astype(
        bf16
    )
    head_table = jnp.asarray(head_selectors(dies), bf16)
    hb = jnp.einsum("tsk,ko->tso", head_table, head_weight, preferred_element_type=f32).astype(
        bf16
    )
    dw = depth_kernel.reshape(blocks, 128, 49).transpose(0, 2, 1)
    center = (jnp.arange(49) == 24).astype(f32)
    dw = jnp.broadcast_to((dw + center[None, :, None])[:, :, None, :], (blocks, 49, 8, 128))
    place = jnp.stack(
        [
            lax.axis_index("ty") * rows,
            lax.axis_index("tx") * cols,
            lax.axis_size("ty") * rows,
            lax.axis_size("tx") * cols,
        ]
    ).astype(jnp.int32)
    cong, bins = network(
        place,
        x,
        xh,
        c,
        ch,
        w1,
        hb,
        dw,
        jnp.swapaxes(down_weight, 1, 2),
        down_weight,
        mix_weight.T,
        mix_weight,
        jnp.swapaxes(up_weight, 1, 2),
        up_weight,
        rows,
        cols,
    )
    congestion = jnp.transpose(cong.reshape(tile_rows, dies, tile_cols), (1, 0, 2))
    halves = tile_cols // 128
    per_die = tile_rows * halves
    block = send_blocks[0]
    die, inside = (block // per_die, block % per_die)
    where = (inside % halves) * (tile_rows * dies) + (inside // halves) * dies + die
    outgoing = bins.reshape(-1, 128).at[where].get(mode="promise_in_bounds")
    received = lax.all_to_all(outgoing, ("ty", "tx"), split_axis=0, concat_axis=0, tiled=True)
    slot_count = received.shape[0]
    slot_hot = (cell_slot[:, None] == jnp.arange(slot_count, dtype=jnp.int32)[None, :]).astype(f32)
    block_rows = jnp.dot(slot_hot, received, precision=lax.Precision.HIGHEST)
    offset_hot = (cell_offset[:, None] == jnp.arange(128, dtype=jnp.int32)[None, :]).astype(f32)
    cell_grad = cell_area * jnp.sum(block_rows * offset_hot, axis=1)
    return (congestion, cell_grad)


def solution(mesh):
    in_specs = (
        P(None, "ty", "tx"),
        P(),
        P(),
        P(),
        P(),
        P(),
        P(),
        P(None, "ty", "tx"),
        P(("ty", "tx"), None),
        P(("ty", "tx")),
        P(("ty", "tx")),
        P(("ty", "tx")),
    )
    out_specs = (P(None, "ty", "tx"), P(("ty", "tx")))
    return jax.shard_map(local, mesh=mesh, in_specs=in_specs, out_specs=out_specs, check_vma=False)
```
